128 devices in a mesh: gx: 8 (over y_hi, x), gy: 4 (over z), gz: 4 (over y_lo, core).
Axes of the slice: x: 4, y: 4 (y_hi: 2, y_lo: 2; y = y_hi * 2 + y_lo), z: 4, core: 2. Of those that a mesh axis runs over, the one named last changes fastest.
Arguments:
- coeffs: float32 [128, 512, 512], P(('gx', 'gy', 'gz')), may hold values from -6 to 6
- transfer: float32 [4, 128, 512, 1024], P(None, ('gx', 'gy', 'gz')), may hold values from -0.1875 to 0.1875
Outputs:
- result: float32 [128, 512, 512], P(('gx', 'gy', 'gz'))
The draws below stay inside these ranges and needn't reach their ends.
All inputs are finite; a program needn't handle non-finite values.
Results may differ from the reference program's by a relative error of at most 0.0001.
Values sent between devices are 32-bit elements; how exact they have to be, the bound alone decides.
A program may use at most 64 MiB of HBM per device.

```python
import jax
import jax.numpy as jnp
from jax import lax

RANK = 512
RHS = 512
LEVELS = 4
BOXES = 128


def block_levels(own_key, dims, cuts, smallest, largest):
    loudness = 1.0
    for axis_at, blocks in cuts:
        steps = jax.random.uniform(jax.random.fold_in(jax.random.fold_in(own_key, 6), axis_at), (blocks,), jnp.float32, smallest / len(cuts), largest / len(cuts))
        loudness = loudness * jnp.repeat(jnp.exp(steps), dims[axis_at] // blocks).reshape((-1,) + (1,) * (len(dims) - 1 - axis_at))
    return loudness


def centred(key, extent, spread, most, cuts=(), dtype=jnp.bfloat16):
    factor_of = block_levels(key, extent, cuts, -0.22, 0.18) if cuts else 1.0
    array = jax.random.normal(key, extent, jnp.float32) * spread * factor_of
    return jnp.minimum(jnp.maximum(array, -most), most).astype(dtype)


def setup_inputs(seed: int = 0) -> dict:
    arg_keys = jax.random.split(jax.random.key(seed), 3)
    return {
        "coeffs": centred(arg_keys[0], (BOXES, RANK, RHS), 1.0, 6.0, ((0, 128),), jnp.float32),
        "transfer": centred(arg_keys[1], (LEVELS, BOXES, RANK, 2 * RANK), (2 * RANK) ** -0.5, 0.1875, ((1, 128),), jnp.float32),
    }


def reference(coeffs, transfer):
    count = coeffs.shape[0]
    nbits = count.bit_length() - 1
    current = coeffs
    for level in range(LEVELS):
        span = 2 ** (nbits - 1 - level)
        grouped = current.reshape(count // (2 * span), 2, span, RANK, RHS)
        paired = jnp.concatenate([grouped[:, 0], grouped[:, 1]], axis=2)
        paired = jnp.stack([paired, paired], axis=1).reshape(count, 2 * RANK, RHS)
        current = jnp.einsum("prs,psk->prk", transfer[level], paired, precision=lax.Precision.HIGHEST)
    return current
```

```python
import functools

import jax
import jax.numpy as jnp
from jax import lax
from jax.experimental import pallas as pl
from jax.experimental.pallas import tpu as pltpu
from jax.sharding import PartitionSpec as P

MESH = pl.DeviceIdType.MESH
LEVELS = 4
RANK = 512
BF16 = jnp.bfloat16
F32 = jnp.float32
AXES = ("gx", "gy", "gz")

CHUNKS = tuple((64 * k, 64) for k in range(8))
ORDER = (
    (0, 0), (0, 1), (0, 2), (1, 0), (0, 3), (1, 1), (0, 4), (1, 2), (2, 0), (0, 5), (0, 6), (1, 3), (2, 1), (3, 0),
    (0, 7), (1, 4), (2, 2), (3, 1), (1, 5), (3, 2), (1, 6), (2, 3), (1, 7), (2, 4), (3, 3), (2, 5), (2, 6), (3, 4),
    (2, 7), (3, 5), (3, 6), (3, 7),
)


def position(level):
    place = [lax.axis_index(a) for a in AXES]
    axis, low = ((0, 4), (0, 2), (0, 1), (1, 2))[level]
    upper = lax.rem(lax.div(place[axis], low), 2)
    place[axis] = place[axis] + low - 2 * low * upper
    return upper, tuple(place)


def split(x):
    high = x.astype(BF16)
    return high, (x - high.astype(F32)).astype(BF16)


def product(rows, high_ref, low_ref):
    high, low = split(rows)
    m = high_ref[...]
    total = jnp.dot(high, m, preferred_element_type=F32)
    total += jnp.dot(low, m, preferred_element_type=F32)
    total += jnp.dot(high, low_ref[...], preferred_element_type=F32)
    return total


def kernel(c_hbm, t_hbm, o_ref, c_in, t_in, high, low, own, other, last, c_sem, t_sem, send_sem, recv_sem):
    groups = [pltpu.make_async_copy(c_hbm.at[:, pl.ds(128 * g, 128)], c_in.at[:, pl.ds(128 * g, 128)], c_sem.at[g]) for g in range(4)]
    loads = [pltpu.make_async_copy(t_hbm.at[l], t_in.at[l], t_sem.at[l]) for l in range(LEVELS)]
    for copy in groups + loads:
        copy.start()

    spots = [position(l) for l in range(LEVELS)]
    barrier = pltpu.get_barrier_semaphore()
    for _, partner in spots:
        pl.semaphore_signal(barrier, inc=1, device_id=partner, device_id_type=MESH)

    def sending(level, chunk):
        first, count = CHUNKS[chunk]
        return pltpu.make_async_remote_copy(
            src_ref=own.at[level, pl.ds(first, count)],
            dst_ref=other.at[level, pl.ds(first, count)],
            send_sem=send_sem.at[level, chunk],
            recv_sem=recv_sem.at[level, chunk],
            device_id=spots[level][1],
            device_id_type=MESH,
        )

    for g in range(4):
        groups[g].wait()
        own[0, pl.ds(128 * g, 128), :] = c_in[:, pl.ds(128 * g, 128)].T
        if g == 0:
            pl.semaphore_wait(barrier, LEVELS)
        for chunk, (first, _) in enumerate(CHUNKS):
            if first // 128 == g:
                sending(0, chunk).start()

    for l in range(LEVELS):
        loads[l].wait()

        def prepare(block, carry):
            r = pl.multiple_of(128 * block, 128)
            for half in range(2):
                m = t_in[l, pl.ds(r, 128), pl.ds(RANK * half, RANK)].T
                h, w = split(m)
                high[l, half, :, pl.ds(r, 128)] = h
                low[l, half, :, pl.ds(r, 128)] = w
            return carry

        lax.fori_loop(0, 4, prepare, 0)

    for level, chunk in ORDER:
        first, count = CHUNKS[chunk]
        rows = pl.ds(first, count)
        upper = spots[level][0]
        total = product(own[level, rows, :], high.at[level, upper], low.at[level, upper])
        sending(level, chunk).wait_recv()
        total += product(other[level, rows, :], high.at[level, 1 - upper], low.at[level, 1 - upper])
        if level + 1 < LEVELS:
            own[level + 1, rows, :] = total
            sending(level + 1, chunk).start()
        else:
            last[rows, :] = total
            if (first + count) % 128 == 0:
                g = (first + count) // 128 - 1
                o_ref[:, pl.ds(128 * g, 128)] = last[pl.ds(128 * g, 128), :].T

    for level in range(LEVELS):
        for chunk in range(len(CHUNKS)):
            sending(level, chunk).wait_send()


def per_device(coeffs, transfer):
    count = len(CHUNKS)
    result = pl.pallas_call(
        kernel,
        out_shape=jax.ShapeDtypeStruct((RANK, RANK), F32),
        in_specs=[pl.BlockSpec(memory_space=pltpu.HBM)] * 2,
        out_specs=pl.BlockSpec(memory_space=pltpu.VMEM),
        scratch_shapes=[
            pltpu.VMEM((RANK, RANK), F32),
            pltpu.VMEM((LEVELS, RANK, 2 * RANK), F32),
            pltpu.VMEM((LEVELS, 2, RANK, RANK), BF16),
            pltpu.VMEM((LEVELS, 2, RANK, RANK), BF16),
            pltpu.VMEM((LEVELS, RANK, RANK), F32),
            pltpu.VMEM((LEVELS, RANK, RANK), F32),
            pltpu.VMEM((RANK, RANK), F32),
            pltpu.SemaphoreType.DMA((4,)),
            pltpu.SemaphoreType.DMA((LEVELS,)),
            pltpu.SemaphoreType.DMA((LEVELS, count)),
            pltpu.SemaphoreType.DMA((LEVELS, count)),
        ],
        compiler_params=pltpu.CompilerParams(collective_id=0, has_side_effects=True, vmem_limit_bytes=48 << 20),
        name="butterfly",
    )(pltpu.with_memory_space_constraint(coeffs[0], pltpu.HBM), transfer[:, 0])
    return result[None]


def solution(mesh):
    return jax.shard_map(
        per_device,
        mesh=mesh,
        in_specs=(P(AXES, None, None), P(None, AXES, None, None)),
        out_specs=P(AXES, None, None),
        check_vma=False,
    )
```

```python
import functools

import jax
import jax.numpy as jnp
from jax import lax
from jax.experimental import pallas as pl
from jax.experimental.pallas import tpu as pltpu
from jax.sharding import PartitionSpec as P

MESH = pl.DeviceIdType.MESH
LEVELS = 4
RANK = 512
BF16 = jnp.bfloat16
F32 = jnp.float32
AXES = ("gx", "gy", "gz")

CHUNKS = (
    (0, 16), (16, 16), (32, 32), (64, 32), (96, 32), (128, 32), (160, 32), (192, 32), (224, 32), (256, 32),
    (288, 32), (320, 32), (352, 32), (384, 32), (416, 32), (448, 32), (480, 16), (496, 16),
)
PREPARE = -1
ORDER = (
    (PREPARE, 1), (0, 0), (0, 1), (PREPARE, 2), (0, 2), (1, 0), (0, 3), (1, 1), (0, 4), (PREPARE, 3), (0, 5),
    (1, 2), (2, 0), (0, 6), (1, 3), (2, 1), (0, 7), (1, 4), (0, 8), (3, 0), (1, 5), (0, 9), (2, 2), (0, 10),
    (3, 1), (1, 6), (0, 11), (2, 3), (0, 12), (3, 2), (1, 7), (0, 13), (2, 4), (0, 14), (3, 3), (1, 8), (0,
    15), (0, 16), (2, 5), (0, 17), (3, 4), (1, 9), (1, 10), (2, 6), (3, 5), (1, 11), (1, 12), (3, 6), (2, 7),
    (1, 13), (1, 14), (2, 8), (3, 7), (1, 15), (1, 16), (1, 17), (3, 8), (2, 9), (2, 10), (2, 11), (2, 12),
    (3, 9), (2, 13), (3, 10), (2, 14), (3, 11), (2, 15), (3, 12), (2, 16), (2, 17), (3, 13), (3, 14), (3, 15),
    (3, 16), (3, 17),
)


def position(level):
    place = [lax.axis_index(a) for a in AXES]
    axis, low = ((0, 4), (0, 2), (0, 1), (1, 2))[level]
    upper = lax.rem(lax.div(place[axis], low), 2)
    place[axis] = place[axis] + low - 2 * low * upper
    return upper, tuple(place)


def split(x):
    high = x.astype(BF16)
    return high, (x - high.astype(F32)).astype(BF16)


def product(rows, high_ref, low_ref):
    high, low = split(rows)
    n = rows.shape[0]
    both = jnp.dot(jnp.concatenate([high, low], axis=0), high_ref[...], preferred_element_type=F32)
    return both[:n] + both[n:] + jnp.dot(high, low_ref[...], preferred_element_type=F32)


def kernel(c_hbm, t_hbm, o_ref, c_in, t_in, high, low, own, other, last, c_sem, t_sem, send_sem, recv_sem):
    groups = [pltpu.make_async_copy(c_hbm.at[:, pl.ds(128 * g, 128)], c_in.at[:, pl.ds(128 * g, 128)], c_sem.at[g]) for g in range(4)]
    loads = [pltpu.make_async_copy(t_hbm.at[l], t_in.at[l], t_sem.at[l]) for l in range(LEVELS)]
    for copy in groups[:1] + loads[:1] + groups[1:] + loads[1:]:
        copy.start()

    spots = [position(l) for l in range(LEVELS)]
    barrier = pltpu.get_barrier_semaphore()
    for _, partner in spots:
        pl.semaphore_signal(barrier, inc=1, device_id=partner, device_id_type=MESH)

    def sending(level, chunk):
        first, count = CHUNKS[chunk]
        return pltpu.make_async_remote_copy(
            src_ref=own.at[level, pl.ds(first, count)],
            dst_ref=other.at[level, pl.ds(first, count)],
            send_sem=send_sem.at[level, chunk],
            recv_sem=recv_sem.at[level, chunk],
            device_id=spots[level][1],
            device_id_type=MESH,
        )

    for g in range(4):
        groups[g].wait()
        own[0, pl.ds(128 * g, 128), :] = c_in[:, pl.ds(128 * g, 128)].T
        if g == 0:
            pl.semaphore_wait(barrier, LEVELS)
        for chunk, (first, _) in enumerate(CHUNKS):
            if first // 128 == g:
                sending(0, chunk).start()

    def prepare(level):
        loads[level].wait()

        def step(block, carry):
            r = pl.multiple_of(128 * block, 128)
            for half in range(2):
                m = t_in[level, pl.ds(r, 128), pl.ds(RANK * half, RANK)].T
                h, w = split(m)
                high[level, half, :, pl.ds(r, 128)] = h
                low[level, half, :, pl.ds(r, 128)] = w
            return carry

        lax.fori_loop(0, 4, step, 0)

    prepare(0)
    for level, chunk in ORDER:
        if level == PREPARE:
            prepare(chunk)
            continue
        first, count = CHUNKS[chunk]
        rows = pl.ds(first, count)
        upper = spots[level][0]
        total = product(own[level, rows, :], high.at[level, upper], low.at[level, upper])
        sending(level, chunk).wait_recv()
        total += product(other[level, rows, :], high.at[level, 1 - upper], low.at[level, 1 - upper])
        if level + 1 < LEVELS:
            own[level + 1, rows, :] = total
            sending(level + 1, chunk).start()
        else:
            last[rows, :] = total
            if (first + count) % 128 == 0:
                g = (first + count) // 128 - 1
                o_ref[:, pl.ds(128 * g, 128)] = last[pl.ds(128 * g, 128), :].T

    for level in range(LEVELS):
        for chunk in range(len(CHUNKS)):
            sending(level, chunk).wait_send()


def per_device(coeffs, transfer):
    count = len(CHUNKS)
    result = pl.pallas_call(
        kernel,
        out_shape=jax.ShapeDtypeStruct((RANK, RANK), F32),
        in_specs=[pl.BlockSpec(memory_space=pltpu.HBM)] * 2,
        out_specs=pl.BlockSpec(memory_space=pltpu.VMEM),
        scratch_shapes=[
            pltpu.VMEM((RANK, RANK), F32),
            pltpu.VMEM((LEVELS, RANK, 2 * RANK), F32),
            pltpu.VMEM((LEVELS, 2, RANK, RANK), BF16),
            pltpu.VMEM((LEVELS, 2, RANK, RANK), BF16),
            pltpu.VMEM((LEVELS, RANK, RANK), F32),
            pltpu.VMEM((LEVELS, RANK, RANK), F32),
            pltpu.VMEM((RANK, RANK), F32),
            pltpu.SemaphoreType.DMA((4,)),
            pltpu.SemaphoreType.DMA((LEVELS,)),
            pltpu.SemaphoreType.DMA((LEVELS, count)),
            pltpu.SemaphoreType.DMA((LEVELS, count)),
        ],
        compiler_params=pltpu.CompilerParams(collective_id=0, has_side_effects=True, vmem_limit_bytes=48 << 20),
        name="butterfly",
    )(pltpu.with_memory_space_constraint(coeffs[0], pltpu.HBM), transfer[:, 0])
    return result[None]


def solution(mesh):
    return jax.shard_map(
        per_device,
        mesh=mesh,
        in_specs=(P(AXES, None, None), P(None, AXES, None, None)),
        out_specs=P(AXES, None, None),
        check_vma=False,
    )
```

```python
import functools

import jax
import jax.numpy as jnp
from jax import lax
from jax.experimental import pallas as pl
from jax.experimental.pallas import tpu as pltpu
from jax.sharding import PartitionSpec as P

MESH = pl.DeviceIdType.MESH
LEVELS = 4
RANK = 512
BF16 = jnp.bfloat16
F32 = jnp.float32
AXES = ("gx", "gy", "gz")

CHUNKS = tuple((32 * k, 32) for k in range(16))
LAGS = (0, 3, 6, 9)


def order():
    for step in range(len(CHUNKS) + LAGS[-1]):
        for level, lag in enumerate(LAGS):
            if 0 <= step - lag < len(CHUNKS):
                yield level, step - lag


def position(level):
    place = [lax.axis_index(a) for a in AXES]
    axis, low = ((0, 4), (0, 2), (0, 1), (1, 2))[level]
    upper = lax.rem(lax.div(place[axis], low), 2)
    place[axis] = place[axis] + low - 2 * low * upper
    return upper, tuple(place)


def split(x):
    high = x.astype(BF16)
    return high, (x - high.astype(F32)).astype(BF16)


def product(rows, high_ref, low_ref):
    high, low = split(rows)
    n = rows.shape[0]
    both = jnp.dot(jnp.concatenate([high, low], axis=0), high_ref[...], preferred_element_type=F32)
    return both[:n] + both[n:] + jnp.dot(high, low_ref[...], preferred_element_type=F32)


def kernel(c_hbm, t_hbm, o_ref, c_in, t_in, high, low, own, other, last, c_sem, t_sem, send_sem, recv_sem):
    groups = [pltpu.make_async_copy(c_hbm.at[:, pl.ds(128 * g, 128)], c_in.at[:, pl.ds(128 * g, 128)], c_sem.at[g]) for g in range(4)]
    loads = [pltpu.make_async_copy(t_hbm.at[l], t_in.at[l], t_sem.at[l]) for l in range(LEVELS)]
    groups[0].start()

    spots = [position(l) for l in range(LEVELS)]
    barrier = pltpu.get_barrier_semaphore()
    for _, partner in spots:
        pl.semaphore_signal(barrier, inc=1, device_id=partner, device_id_type=MESH)
    for copy in loads[:1] + groups[1:] + loads[1:]:
        copy.start()

    def sending(level, chunk):
        first, count = CHUNKS[chunk]
        return pltpu.make_async_remote_copy(
            src_ref=own.at[level, pl.ds(first, count)],
            dst_ref=other.at[level, pl.ds(first, count)],
            send_sem=send_sem.at[level, chunk],
            recv_sem=recv_sem.at[level, chunk],
            device_id=spots[level][1],
            device_id_type=MESH,
        )

    for g in range(4):
        groups[g].wait()
        own[0, pl.ds(128 * g, 128), :] = c_in[:, pl.ds(128 * g, 128)].T
        if g == 0:
            pl.semaphore_wait(barrier, LEVELS)
        for chunk, (first, _) in enumerate(CHUNKS):
            if first // 128 == g:
                sending(0, chunk).start()

    def prepare(level):
        loads[level].wait()

        def step(block, carry):
            r = pl.multiple_of(128 * block, 128)
            for half in range(2):
                m = t_in[level, pl.ds(r, 128), pl.ds(RANK * half, RANK)].T
                h, w = split(m)
                high[level, half, :, pl.ds(r, 128)] = h
                low[level, half, :, pl.ds(r, 128)] = w
            return carry

        lax.fori_loop(0, 4, step, 0)

    prepare(0)
    prepare(1)
    for level, chunk in order():
        if (level, chunk) in ((0, 2), (0, 3)):
            prepare(chunk)
        first, count = CHUNKS[chunk]
        rows = pl.ds(first, count)
        upper = spots[level][0]
        total = product(own[level, rows, :], high.at[level, upper], low.at[level, upper])
        sending(level, chunk).wait_recv()
        total += product(other[level, rows, :], high.at[level, 1 - upper], low.at[level, 1 - upper])
        if level + 1 < LEVELS:
            own[level + 1, rows, :] = total
            sending(level + 1, chunk).start()
        else:
            last[rows, :] = total
            if (first + count) % 128 == 0:
                g = (first + count) // 128 - 1
                o_ref[:, pl.ds(128 * g, 128)] = last[pl.ds(128 * g, 128), :].T

    for level in range(LEVELS):
        for chunk in range(len(CHUNKS)):
            sending(level, chunk).wait_send()


def per_device(coeffs, transfer):
    count = len(CHUNKS)
    result = pl.pallas_call(
        kernel,
        out_shape=jax.ShapeDtypeStruct((RANK, RANK), F32),
        in_specs=[pl.BlockSpec(memory_space=pltpu.HBM)] * 2,
        out_specs=pl.BlockSpec(memory_space=pltpu.VMEM),
        scratch_shapes=[
            pltpu.VMEM((RANK, RANK), F32),
            pltpu.VMEM((LEVELS, RANK, 2 * RANK), F32),
            pltpu.VMEM((LEVELS, 2, RANK, RANK), BF16),
            pltpu.VMEM((LEVELS, 2, RANK, RANK), BF16),
            pltpu.VMEM((LEVELS, RANK, RANK), F32),
            pltpu.VMEM((LEVELS, RANK, RANK), F32),
            pltpu.VMEM((RANK, RANK), F32),
            pltpu.SemaphoreType.DMA((4,)),
            pltpu.SemaphoreType.DMA((LEVELS,)),
            pltpu.SemaphoreType.DMA((LEVELS, count)),
            pltpu.SemaphoreType.DMA((LEVELS, count)),
        ],
        compiler_params=pltpu.CompilerParams(collective_id=0, has_side_effects=True, vmem_limit_bytes=48 << 20),
        name="butterfly",
    )(pltpu.with_memory_space_constraint(coeffs[0], pltpu.HBM), transfer[:, 0])
    return result[None]


def solution(mesh):
    return jax.shard_map(
        per_device,
        mesh=mesh,
        in_specs=(P(AXES, None, None), P(None, AXES, None, None)),
        out_specs=P(AXES, None, None),
        check_vma=False,
    )
```

```python
import functools

import jax
import jax.numpy as jnp
from jax import lax
from jax.experimental import pallas as pl
from jax.experimental.pallas import tpu as pltpu
from jax.sharding import PartitionSpec as P

MESH = pl.DeviceIdType.MESH
LEVELS = 4
RANK = 512
BF16 = jnp.bfloat16
F32 = jnp.float32
AXES = ("gx", "gy", "gz")

CHUNKS = tuple((48 * k, min(48, 512 - 48 * k)) for k in range(11))
LAGS = (0, 2, 4, 7)


def order():
    for step in range(len(CHUNKS) + LAGS[-1]):
        for level, lag in enumerate(LAGS):
            if 0 <= step - lag < len(CHUNKS):
                yield level, step - lag


def position(level):
    place = [lax.axis_index(a) for a in AXES]
    axis, low = ((0, 4), (0, 2), (0, 1), (1, 2))[level]
    upper = lax.rem(lax.div(place[axis], low), 2)
    place[axis] = place[axis] + low - 2 * low * upper
    return upper, tuple(place)


def split(x):
    high = x.astype(BF16)
    return high, (x - high.astype(F32)).astype(BF16)


def product(rows, high_ref, low_ref):
    high, low = split(rows)
    n = rows.shape[0]
    both = jnp.dot(jnp.concatenate([high, low], axis=0), high_ref[...], preferred_element_type=F32)
    return both[:n] + both[n:] + jnp.dot(high, low_ref[...], preferred_element_type=F32)


def kernel(c_hbm, t_hbm, o_ref, c_in, t_in, high, low, own, other, last, c_sem, t_sem, send_sem, recv_sem):
    groups = [pltpu.make_async_copy(c_hbm.at[:, pl.ds(128 * g, 128)], c_in.at[:, pl.ds(128 * g, 128)], c_sem.at[g]) for g in range(4)]
    loads = [pltpu.make_async_copy(t_hbm.at[l], t_in.at[l], t_sem.at[l]) for l in range(LEVELS)]
    groups[0].start()

    spots = [position(l) for l in range(LEVELS)]
    barrier = pltpu.get_barrier_semaphore()
    for _, partner in spots:
        pl.semaphore_signal(barrier, inc=1, device_id=partner, device_id_type=MESH)
    for copy in loads[:1] + groups[1:] + loads[1:]:
        copy.start()

    def sending(level, chunk):
        first, count = CHUNKS[chunk]
        return pltpu.make_async_remote_copy(
            src_ref=own.at[level, pl.ds(first, count)],
            dst_ref=other.at[level, pl.ds(first, count)],
            send_sem=send_sem.at[level, chunk],
            recv_sem=recv_sem.at[level, chunk],
            device_id=spots[level][1],
            device_id_type=MESH,
        )

    for g in range(4):
        groups[g].wait()
        own[0, pl.ds(128 * g, 128), :] = c_in[:, pl.ds(128 * g, 128)].T
        if g == 0:
            pl.semaphore_wait(barrier, LEVELS)
        for chunk, (first, count) in enumerate(CHUNKS):
            if (first + count - 1) // 128 == g:
                sending(0, chunk).start()

    def prepare(level):
        loads[level].wait()

        def step(block, carry):
            r = pl.multiple_of(128 * block, 128)
            for half in range(2):
                m = t_in[level, pl.ds(r, 128), pl.ds(RANK * half, RANK)].T
                h, w = split(m)
                high[level, half, :, pl.ds(r, 128)] = h
                low[level, half, :, pl.ds(r, 128)] = w
            return carry

        lax.fori_loop(0, 4, step, 0)

    prepare(0)
    prepare(1)
    for level, chunk in order():
        if (level, chunk) in ((0, 1), (0, 2)):
            prepare(chunk + 1)
        first, count = CHUNKS[chunk]
        rows = pl.ds(first, count)
        upper = spots[level][0]
        total = product(own[level, rows, :], high.at[level, upper], low.at[level, upper])
        sending(level, chunk).wait_recv()
        total += product(other[level, rows, :], high.at[level, 1 - upper], low.at[level, 1 - upper])
        if level + 1 < LEVELS:
            own[level + 1, rows, :] = total
            sending(level + 1, chunk).start()
        else:
            last[rows, :] = total
            if (first + count) // 128 > first // 128:
                g = (first + count) // 128 - 1
                o_ref[:, pl.ds(128 * g, 128)] = last[pl.ds(128 * g, 128), :].T

    for level in range(LEVELS):
        for chunk in range(len(CHUNKS)):
            sending(level, chunk).wait_send()


def per_device(coeffs, transfer):
    count = len(CHUNKS)
    result = pl.pallas_call(
        kernel,
        out_shape=jax.ShapeDtypeStruct((RANK, RANK), F32),
        in_specs=[pl.BlockSpec(memory_space=pltpu.HBM)] * 2,
        out_specs=pl.BlockSpec(memory_space=pltpu.VMEM),
        scratch_shapes=[
            pltpu.VMEM((RANK, RANK), F32),
            pltpu.VMEM((LEVELS, RANK, 2 * RANK), F32),
            pltpu.VMEM((LEVELS, 2, RANK, RANK), BF16),
            pltpu.VMEM((LEVELS, 2, RANK, RANK), BF16),
            pltpu.VMEM((LEVELS, RANK, RANK), F32),
            pltpu.VMEM((LEVELS, RANK, RANK), F32),
            pltpu.VMEM((RANK, RANK), F32),
            pltpu.SemaphoreType.DMA((4,)),
            pltpu.SemaphoreType.DMA((LEVELS,)),
            pltpu.SemaphoreType.DMA((LEVELS, count)),
            pltpu.SemaphoreType.DMA((LEVELS, count)),
        ],
        compiler_params=pltpu.CompilerParams(collective_id=0, has_side_effects=True, vmem_limit_bytes=48 << 20),
        name="butterfly",
    )(pltpu.with_memory_space_constraint(coeffs[0], pltpu.HBM), transfer[:, 0])
    return result[None]


def solution(mesh):
    return jax.shard_map(
        per_device,
        mesh=mesh,
        in_specs=(P(AXES, None, None), P(None, AXES, None, None)),
        out_specs=P(AXES, None, None),
        check_vma=False,
    )
```

```python
import functools

import jax
import jax.numpy as jnp
from jax import lax
from jax.experimental import pallas as pl
from jax.experimental.pallas import tpu as pltpu
from jax.sharding import PartitionSpec as P

MESH = pl.DeviceIdType.MESH
LEVELS = 4
RANK = 512
BF16 = jnp.bfloat16
F32 = jnp.float32
AXES = ("gx", "gy", "gz")

GROUPS = ((16, 32),) + 9 * ((48,),) + ((16, 16),)
WIDTHS = sum(GROUPS, ())
CHUNKS = tuple((sum(WIDTHS[:k]), WIDTHS[k]) for k in range(len(WIDTHS)))
LAGS = (0, 2, 4, 7)


def order():
    for step in range(len(GROUPS) + LAGS[-1]):
        for level, lag in enumerate(LAGS):
            group = step - lag
            if 0 <= group < len(GROUPS):
                first = sum(map(len, GROUPS[:group]))
                for chunk in range(first, first + len(GROUPS[group])):
                    yield level, chunk, group


def position(level):
    place = [lax.axis_index(a) for a in AXES]
    axis, low = ((0, 4), (0, 2), (0, 1), (1, 2))[level]
    upper = lax.rem(lax.div(place[axis], low), 2)
    place[axis] = place[axis] + low - 2 * low * upper
    return upper, tuple(place)


def split(x):
    high = x.astype(BF16)
    return high, (x - high.astype(F32)).astype(BF16)


def product(rows, high_ref, low_ref):
    high, low = split(rows)
    n = rows.shape[0]
    both = jnp.dot(jnp.concatenate([high, low], axis=0), high_ref[...], preferred_element_type=F32)
    return both[:n] + both[n:] + jnp.dot(high, low_ref[...], preferred_element_type=F32)


def kernel(c_hbm, t_hbm, o_ref, c_in, t_in, high, low, own, other, last, c_sem, t_sem, send_sem, recv_sem):
    groups = [pltpu.make_async_copy(c_hbm.at[:, pl.ds(128 * g, 128)], c_in.at[:, pl.ds(128 * g, 128)], c_sem.at[g]) for g in range(4)]
    loads = [pltpu.make_async_copy(t_hbm.at[l], t_in.at[l], t_sem.at[l]) for l in range(LEVELS)]
    groups[0].start()

    spots = [position(l) for l in range(LEVELS)]
    barrier = pltpu.get_barrier_semaphore()
    for _, partner in spots:
        pl.semaphore_signal(barrier, inc=1, device_id=partner, device_id_type=MESH)
    for copy in loads[:1] + groups[1:] + loads[1:]:
        copy.start()

    def sending(level, chunk):
        first, count = CHUNKS[chunk]
        return pltpu.make_async_remote_copy(
            src_ref=own.at[level, pl.ds(first, count)],
            dst_ref=other.at[level, pl.ds(first, count)],
            send_sem=send_sem.at[level, chunk],
            recv_sem=recv_sem.at[level, chunk],
            device_id=spots[level][1],
            device_id_type=MESH,
        )

    for g in range(4):
        groups[g].wait()
        own[0, pl.ds(128 * g, 128), :] = c_in[:, pl.ds(128 * g, 128)].T
        if g == 0:
            pl.semaphore_wait(barrier, LEVELS)
        for chunk, (first, count) in enumerate(CHUNKS):
            if (first + count - 1) // 128 == g:
                sending(0, chunk).start()

    def prepare(level):
        loads[level].wait()

        def step(block, carry):
            r = pl.multiple_of(128 * block, 128)
            for half in range(2):
                m = t_in[level, pl.ds(r, 128), pl.ds(RANK * half, RANK)].T
                h, w = split(m)
                high[level, half, :, pl.ds(r, 128)] = h
                low[level, half, :, pl.ds(r, 128)] = w
            return carry

        lax.fori_loop(0, 4, step, 0)

    prepare(0)
    prepare(1)
    for level, chunk, group in order():
        if (level, group) in ((0, 1), (0, 2)):
            prepare(group + 1)
        first, count = CHUNKS[chunk]
        rows = pl.ds(first, count)
        upper = spots[level][0]
        total = product(own[level, rows, :], high.at[level, upper], low.at[level, upper])
        sending(level, chunk).wait_recv()
        total += product(other[level, rows, :], high.at[level, 1 - upper], low.at[level, 1 - upper])
        if level + 1 < LEVELS:
            own[level + 1, rows, :] = total
            sending(level + 1, chunk).start()
        else:
            last[rows, :] = total
            if (first + count) // 128 > first // 128:
                g = (first + count) // 128 - 1
                o_ref[:, pl.ds(128 * g, 128)] = last[pl.ds(128 * g, 128), :].T

    for level in range(LEVELS):
        for chunk in range(len(CHUNKS)):
            sending(level, chunk).wait_send()


def per_device(coeffs, transfer):
    count = len(CHUNKS)
    result = pl.pallas_call(
        kernel,
        out_shape=jax.ShapeDtypeStruct((RANK, RANK), F32),
        in_specs=[pl.BlockSpec(memory_space=pltpu.HBM)] * 2,
        out_specs=pl.BlockSpec(memory_space=pltpu.VMEM),
        scratch_shapes=[
            pltpu.VMEM((RANK, RANK), F32),
            pltpu.VMEM((LEVELS, RANK, 2 * RANK), F32),
            pltpu.VMEM((LEVELS, 2, RANK, RANK), BF16),
            pltpu.VMEM((LEVELS, 2, RANK, RANK), BF16),
            pltpu.VMEM((LEVELS, RANK, RANK), F32),
            pltpu.VMEM((LEVELS, RANK, RANK), F32),
            pltpu.VMEM((RANK, RANK), F32),
            pltpu.SemaphoreType.DMA((4,)),
            pltpu.SemaphoreType.DMA((LEVELS,)),
            pltpu.SemaphoreType.DMA((LEVELS, count)),
            pltpu.SemaphoreType.DMA((LEVELS, count)),
        ],
        compiler_params=pltpu.CompilerParams(collective_id=0, has_side_effects=True, vmem_limit_bytes=48 << 20),
        name="butterfly",
    )(pltpu.with_memory_space_constraint(coeffs[0], pltpu.HBM), transfer[:, 0])
    return result[None]


def solution(mesh):
    return jax.shard_map(
        per_device,
        mesh=mesh,
        in_specs=(P(AXES, None, None), P(None, AXES, None, None)),
        out_specs=P(AXES, None, None),
        check_vma=False,
    )
```

```python
import functools

import jax
import jax.numpy as jnp
from jax import lax
from jax.experimental import pallas as pl
from jax.experimental.pallas import tpu as pltpu
from jax.sharding import PartitionSpec as P

MESH = pl.DeviceIdType.MESH
LEVELS = 4
RANK = 512
BF16 = jnp.bfloat16
F32 = jnp.float32
AXES = ("gx", "gy", "gz")

CHUNKS = tuple((48 * k, min(48, 512 - 48 * k)) for k in range(11))
LAGS = (0, 2, 4, 7)


def order():
    for step in range(len(CHUNKS) + LAGS[-1]):
        for level, lag in enumerate(LAGS):
            if 0 <= step - lag < len(CHUNKS):
                yield level, step - lag


def position(level):
    place = [lax.axis_index(a) for a in AXES]
    axis, low = ((0, 4), (0, 2), (0, 1), (1, 2))[level]
    upper = lax.rem(lax.div(place[axis], low), 2)
    place[axis] = place[axis] + low - 2 * low * upper
    return upper, tuple(place)


def split(x):
    high = x.astype(BF16)
    return high, (x - high.astype(F32)).astype(BF16)


def product(rows, high_ref, low_ref):
    high, low = split(rows)
    n = rows.shape[0]
    both = jnp.dot(jnp.concatenate([high, low], axis=0), high_ref[...], preferred_element_type=F32)
    return both[:n] + both[n:] + jnp.dot(high, low_ref[...], preferred_element_type=F32)


def kernel(c_hbm, t_hbm, o_ref, c_in, t_in, high, low, own, other, last, c_sem, t_sem, send_sem, recv_sem):
    groups = [pltpu.make_async_copy(c_hbm.at[:, pl.ds(128 * g, 128)], c_in.at[:, pl.ds(128 * g, 128)], c_sem.at[g]) for g in range(4)]
    loads = [pltpu.make_async_copy(t_hbm.at[l], t_in.at[l], t_sem.at[l]) for l in range(LEVELS)]
    groups[0].start()

    spots = [position(l) for l in range(LEVELS)]
    barrier = pltpu.get_barrier_semaphore()
    for _, partner in spots:
        pl.semaphore_signal(barrier, inc=1, device_id=partner, device_id_type=MESH)
    for copy in loads[:1] + groups[1:] + loads[1:]:
        copy.start()

    def sending(level, chunk):
        first, count = CHUNKS[chunk]
        return pltpu.make_async_remote_copy(
            src_ref=own.at[level, pl.ds(first, count)],
            dst_ref=other.at[level, pl.ds(first, count)],
            send_sem=send_sem.at[level, chunk],
            recv_sem=recv_sem.at[level, chunk],
            device_id=spots[level][1],
            device_id_type=MESH,
        )

    core = lax.rem(lax.axis_index("gz"), 2)

    def send_first(g):
        for chunk, (first, count) in enumerate(CHUNKS):
            if (first + count - 1) // 128 == g:
                sending(0, chunk).start()

    for g in range(4):
        groups[g].wait()
        own[0, pl.ds(128 * g, 128), :] = c_in[:, pl.ds(128 * g, 128)].T
        if g == 0:
            pl.semaphore_wait(barrier, LEVELS)
        pl.when(core == 0)(functools.partial(send_first, g))

    def prepare(level):
        loads[level].wait()

        def step(block, carry):
            r = pl.multiple_of(128 * block, 128)
            for half in range(2):
                m = t_in[level, pl.ds(r, 128), pl.ds(RANK * half, RANK)].T
                h, w = split(m)
                high[level, half, :, pl.ds(r, 128)] = h
                low[level, half, :, pl.ds(r, 128)] = w
            return carry

        lax.fori_loop(0, 4, step, 0)

    prepare(0)

    @pl.when(core == 1)
    def _():
        for g in range(4):
            send_first(g)

    prepare(1)
    for level, chunk in order():
        if (level, chunk) in ((0, 1), (0, 2)):
            prepare(chunk + 1)
        first, count = CHUNKS[chunk]
        rows = pl.ds(first, count)
        upper = spots[level][0]
        total = product(own[level, rows, :], high.at[level, upper], low.at[level, upper])
        sending(level, chunk).wait_recv()
        total += product(other[level, rows, :], high.at[level, 1 - upper], low.at[level, 1 - upper])
        if level + 1 < LEVELS:
            own[level + 1, rows, :] = total
            sending(level + 1, chunk).start()
        else:
            last[rows, :] = total
            if (first + count) // 128 > first // 128:
                g = (first + count) // 128 - 1
                o_ref[:, pl.ds(128 * g, 128)] = last[pl.ds(128 * g, 128), :].T

    for level in range(LEVELS):
        for chunk in range(len(CHUNKS)):
            sending(level, chunk).wait_send()


def per_device(coeffs, transfer):
    count = len(CHUNKS)
    result = pl.pallas_call(
        kernel,
        out_shape=jax.ShapeDtypeStruct((RANK, RANK), F32),
        in_specs=[pl.BlockSpec(memory_space=pltpu.HBM)] * 2,
        out_specs=pl.BlockSpec(memory_space=pltpu.VMEM),
        scratch_shapes=[
            pltpu.VMEM((RANK, RANK), F32),
            pltpu.VMEM((LEVELS, RANK, 2 * RANK), F32),
            pltpu.VMEM((LEVELS, 2, RANK, RANK), BF16),
            pltpu.VMEM((LEVELS, 2, RANK, RANK), BF16),
            pltpu.VMEM((LEVELS, RANK, RANK), F32),
            pltpu.VMEM((LEVELS, RANK, RANK), F32),
            pltpu.VMEM((RANK, RANK), F32),
            pltpu.SemaphoreType.DMA((4,)),
            pltpu.SemaphoreType.DMA((LEVELS,)),
            pltpu.SemaphoreType.DMA((LEVELS, count)),
            pltpu.SemaphoreType.DMA((LEVELS, count)),
        ],
        compiler_params=pltpu.CompilerParams(collective_id=0, has_side_effects=True, vmem_limit_bytes=48 << 20),
        name="butterfly",
    )(pltpu.with_memory_space_constraint(coeffs[0], pltpu.HBM), transfer[:, 0])
    return result[None]


def solution(mesh):
    return jax.shard_map(
        per_device,
        mesh=mesh,
        in_specs=(P(AXES, None, None), P(None, AXES, None, None)),
        out_specs=P(AXES, None, None),
        check_vma=False,
    )
```

```python
import functools

import jax
import jax.numpy as jnp
from jax import lax
from jax.experimental import pallas as pl
from jax.experimental.pallas import tpu as pltpu
from jax.sharding import PartitionSpec as P

MESH = pl.DeviceIdType.MESH
LEVELS = 4
RANK = 512
BF16 = jnp.bfloat16
F32 = jnp.float32
AXES = ("gx", "gy", "gz")

CHUNKS = tuple((48 * k, min(48, 512 - 48 * k)) for k in range(11))
LAGS = (0, 2, 4, 7)


def order():
    for step in range(len(CHUNKS) + LAGS[-1]):
        for level, lag in enumerate(LAGS):
            if 0 <= step - lag < len(CHUNKS):
                yield level, step - lag


def position(level):
    place = [lax.axis_index(a) for a in AXES]
    axis, low = ((0, 4), (0, 2), (0, 1), (1, 2))[level]
    upper = lax.rem(lax.div(place[axis], low), 2)
    place[axis] = place[axis] + low - 2 * low * upper
    return upper, tuple(place)


def split(x):
    high = x.astype(BF16)
    return high, (x - high.astype(F32)).astype(BF16)


def product(rows, high_ref, low_ref):
    high, low = split(rows)
    n = rows.shape[0]
    both = jnp.dot(jnp.concatenate([high, low], axis=0), high_ref[...], preferred_element_type=F32)
    return both[:n] + both[n:] + jnp.dot(high, low_ref[...], preferred_element_type=F32)


def kernel(c_hbm, t_hbm, o_ref, c_in, t_in, high, low, own, other, last, c_sem, t_sem, send_sem, recv_sem):
    groups = [pltpu.make_async_copy(c_hbm.at[:, pl.ds(128 * g, 128)], c_in.at[:, pl.ds(128 * g, 128)], c_sem.at[g]) for g in range(4)]
    loads = [pltpu.make_async_copy(t_hbm.at[l], t_in.at[l], t_sem.at[l]) for l in range(LEVELS)]
    groups[0].start()

    spots = [position(l) for l in range(LEVELS)]
    barrier = pltpu.get_barrier_semaphore()
    for _, partner in spots:
        pl.semaphore_signal(barrier, inc=1, device_id=partner, device_id_type=MESH)
    for copy in loads[:1] + groups[1:] + loads[1:]:
        copy.start()

    def sending(level, chunk):
        first, count = CHUNKS[chunk]
        return pltpu.make_async_remote_copy(
            src_ref=own.at[level, pl.ds(first, count)],
            dst_ref=other.at[level, pl.ds(first, count)],
            send_sem=send_sem.at[level, chunk],
            recv_sem=recv_sem.at[level, chunk],
            device_id=spots[level][1],
            device_id_type=MESH,
        )

    for g in range(4):
        groups[g].wait()
        own[0, pl.ds(128 * g, 128), :] = c_in[:, pl.ds(128 * g, 128)].T
        if g == 0:
            pl.semaphore_wait(barrier, LEVELS)
        for chunk, (first, count) in enumerate(CHUNKS):
            if (first + count - 1) // 128 == g:
                sending(0, chunk).start()

    def prepare(level):
        loads[level].wait()

        def step(block, carry):
            r = pl.multiple_of(128 * block, 128)
            for half in range(2):
                m = t_in[level, pl.ds(r, 128), pl.ds(RANK * half, RANK)].T
                h, w = split(m)
                high[level, half, :, pl.ds(r, 128)] = h
                low[level, half, :, pl.ds(r, 128)] = w
            return carry

        lax.fori_loop(0, 4, step, 0)

    prepare(0)
    prepare(1)
    for level, chunk in order():
        if (level, chunk) in ((0, 1), (0, 2)):
            prepare(chunk + 1)
        first, count = CHUNKS[chunk]
        rows = pl.ds(first, count)
        upper = spots[level][0]
        total = product(own[level, rows, :], high.at[level, upper], low.at[level, upper])
        sending(level, chunk).wait_recv()
        total += product(other[level, rows, :], high.at[level, 1 - upper], low.at[level, 1 - upper])
        if level + 1 < LEVELS:
            own[level + 1, rows, :] = total
            sending(level + 1, chunk).start()
        else:
            last[rows, :] = total
            if (first + count) // 128 > first // 128:
                g = (first + count) // 128 - 1
                o_ref[:, pl.ds(128 * g, 128)] = last[pl.ds(128 * g, 128), :].T

    for level in range(LEVELS):
        for chunk in range(len(CHUNKS)):
            sending(level, chunk).wait_send()


def write_out(in_ref, o_hbm, sem):
    copies = [pltpu.make_async_copy(in_ref.at[pl.ds(64 * i, 64)], o_hbm.at[pl.ds(64 * i, 64)], sem.at[i]) for i in range(8)]
    for copy in copies:
        copy.start()
    for copy in copies:
        copy.wait()


def per_device(coeffs, transfer):
    count = len(CHUNKS)
    result = pl.pallas_call(
        kernel,
        out_shape=jax.ShapeDtypeStruct((RANK, RANK), F32),
        in_specs=[pl.BlockSpec(memory_space=pltpu.HBM)] * 2,
        out_specs=pl.BlockSpec(memory_space=pltpu.VMEM),
        scratch_shapes=[
            pltpu.VMEM((RANK, RANK), F32),
            pltpu.VMEM((LEVELS, RANK, 2 * RANK), F32),
            pltpu.VMEM((LEVELS, 2, RANK, RANK), BF16),
            pltpu.VMEM((LEVELS, 2, RANK, RANK), BF16),
            pltpu.VMEM((LEVELS, RANK, RANK), F32),
            pltpu.VMEM((LEVELS, RANK, RANK), F32),
            pltpu.VMEM((RANK, RANK), F32),
            pltpu.SemaphoreType.DMA((4,)),
            pltpu.SemaphoreType.DMA((LEVELS,)),
            pltpu.SemaphoreType.DMA((LEVELS, count)),
            pltpu.SemaphoreType.DMA((LEVELS, count)),
        ],
        compiler_params=pltpu.CompilerParams(collective_id=0, has_side_effects=True, vmem_limit_bytes=48 << 20),
        name="butterfly",
    )(pltpu.with_memory_space_constraint(coeffs[0], pltpu.HBM), transfer[:, 0])
    return pl.pallas_call(
        write_out,
        out_shape=jax.ShapeDtypeStruct((RANK, RANK), F32),
        in_specs=[pl.BlockSpec(memory_space=pltpu.VMEM)],
        out_specs=pl.BlockSpec(memory_space=pltpu.HBM),
        scratch_shapes=[pltpu.SemaphoreType.DMA((8,))],
        compiler_params=pltpu.CompilerParams(vmem_limit_bytes=4 << 20),
        name="write_out",
    )(result)[None]


def solution(mesh):
    return jax.shard_map(
        per_device,
        mesh=mesh,
        in_specs=(P(AXES, None, None), P(None, AXES, None, None)),
        out_specs=P(AXES, None, None),
        check_vma=False,
    )
```

```python
import functools

import jax
import jax.numpy as jnp
from jax import lax
from jax.experimental import pallas as pl
from jax.experimental.pallas import tpu as pltpu
from jax.sharding import PartitionSpec as P

MESH = pl.DeviceIdType.MESH
LEVELS = 4
RANK = 512
BF16 = jnp.bfloat16
F32 = jnp.float32
AXES = ("gx", "gy", "gz")

CHUNKS = tuple((48 * k, min(48, 512 - 48 * k)) for k in range(11))
LAGS = (0, 2, 4, 8)


def order():
    for step in range(len(CHUNKS) + LAGS[-1]):
        for level, lag in enumerate(LAGS):
            if 0 <= step - lag < len(CHUNKS):
                yield level, step - lag


def position(level):
    place = [lax.axis_index(a) for a in AXES]
    axis, low = ((0, 4), (0, 2), (0, 1), (1, 2))[level]
    upper = lax.rem(lax.div(place[axis], low), 2)
    place[axis] = place[axis] + low - 2 * low * upper
    return upper, tuple(place)


def split(x):
    high = x.astype(BF16)
    return high, (x - high.astype(F32)).astype(BF16)


def product(rows, high_ref, low_ref):
    high, low = split(rows)
    n = rows.shape[0]
    both = jnp.dot(jnp.concatenate([high, low], axis=0), high_ref[...], preferred_element_type=F32)
    return both[:n] + both[n:] + jnp.dot(high, low_ref[...], preferred_element_type=F32)


def kernel(c_hbm, t_hbm, o_ref, c_in, t_in, high, low, own, other, last, c_sem, t_sem, send_sem, recv_sem):
    groups = [pltpu.make_async_copy(c_hbm.at[:, pl.ds(128 * g, 128)], c_in.at[:, pl.ds(128 * g, 128)], c_sem.at[g]) for g in range(4)]
    loads = [pltpu.make_async_copy(t_hbm.at[l], t_in.at[l], t_sem.at[l]) for l in range(LEVELS)]
    groups[0].start()

    spots = [position(l) for l in range(LEVELS)]
    barrier = pltpu.get_barrier_semaphore()
    for _, partner in spots:
        pl.semaphore_signal(barrier, inc=1, device_id=partner, device_id_type=MESH)
    for copy in loads[:1] + groups[1:] + loads[1:]:
        copy.start()

    def sending(level, chunk):
        first, count = CHUNKS[chunk]
        return pltpu.make_async_remote_copy(
            src_ref=own.at[level, pl.ds(first, count)],
            dst_ref=other.at[level, pl.ds(first, count)],
            send_sem=send_sem.at[level, chunk],
            recv_sem=recv_sem.at[level, chunk],
            device_id=spots[level][1],
            device_id_type=MESH,
        )

    for g in range(4):
        groups[g].wait()
        own[0, pl.ds(128 * g, 128), :] = c_in[:, pl.ds(128 * g, 128)].T
        if g == 0:
            pl.semaphore_wait(barrier, LEVELS)
        for chunk, (first, count) in enumerate(CHUNKS):
            if (first + count - 1) // 128 == g:
                sending(0, chunk).start()

    def prepare(level):
        loads[level].wait()

        def step(block, carry):
            r = pl.multiple_of(128 * block, 128)
            for half in range(2):
                m = t_in[level, pl.ds(r, 128), pl.ds(RANK * half, RANK)].T
                h, w = split(m)
                high[level, half, :, pl.ds(r, 128)] = h
                low[level, half, :, pl.ds(r, 128)] = w
            return carry

        lax.fori_loop(0, 4, step, 0)

    prepare(0)
    prepare(1)
    for level, chunk in order():
        if (level, chunk) in ((0, 1), (0, 2)):
            prepare(chunk + 1)
        first, count = CHUNKS[chunk]
        rows = pl.ds(first, count)
        upper = spots[level][0]
        total = product(own[level, rows, :], high.at[level, upper], low.at[level, upper])
        sending(level, chunk).wait_recv()
        total += product(other[level, rows, :], high.at[level, 1 - upper], low.at[level, 1 - upper])
        if level + 1 < LEVELS:
            own[level + 1, rows, :] = total
            sending(level + 1, chunk).start()
        else:
            last[rows, :] = total
            if (first + count) // 128 > first // 128:
                g = (first + count) // 128 - 1
                o_ref[:, pl.ds(128 * g, 128)] = last[pl.ds(128 * g, 128), :].T

    for level in range(LEVELS):
        for chunk in range(len(CHUNKS)):
            sending(level, chunk).wait_send()


def per_device(coeffs, transfer):
    count = len(CHUNKS)
    result = pl.pallas_call(
        kernel,
        out_shape=jax.ShapeDtypeStruct((RANK, RANK), F32),
        in_specs=[pl.BlockSpec(memory_space=pltpu.HBM)] * 2,
        out_specs=pl.BlockSpec(memory_space=pltpu.VMEM),
        scratch_shapes=[
            pltpu.VMEM((RANK, RANK), F32),
            pltpu.VMEM((LEVELS, RANK, 2 * RANK), F32),
            pltpu.VMEM((LEVELS, 2, RANK, RANK), BF16),
            pltpu.VMEM((LEVELS, 2, RANK, RANK), BF16),
            pltpu.VMEM((LEVELS, RANK, RANK), F32),
            pltpu.VMEM((LEVELS, RANK, RANK), F32),
            pltpu.VMEM((RANK, RANK), F32),
            pltpu.SemaphoreType.DMA((4,)),
            pltpu.SemaphoreType.DMA((LEVELS,)),
            pltpu.SemaphoreType.DMA((LEVELS, count)),
            pltpu.SemaphoreType.DMA((LEVELS, count)),
        ],
        compiler_params=pltpu.CompilerParams(collective_id=0, has_side_effects=True, vmem_limit_bytes=48 << 20),
        name="butterfly",
    )(pltpu.with_memory_space_constraint(coeffs[0], pltpu.HBM), transfer[:, 0])
    return result[None]


def solution(mesh):
    return jax.shard_map(
        per_device,
        mesh=mesh,
        in_specs=(P(AXES, None, None), P(None, AXES, None, None)),
        out_specs=P(AXES, None, None),
        check_vma=False,
    )
```
